256 devices in a mesh: slab: 32 (over z_lo, x, core), rep: 8 (over z_hi, y).
Axes of the slice: x: 4, y: 4, z: 8 (z_hi: 2, z_lo: 4; z = z_hi * 4 + z_lo), core: 2. Of those that a mesh axis runs over, the one named last changes fastest.
Arguments:
- features: bfloat16 [8, 96, 64, 4, 256], P('rep', None, 'slab'), may hold values from -6 to 6
- occupancy: int32 [8, 64, 4, 256], P('rep', 'slab'), may hold values from 0 to 1, as said below
- w_fine: bfloat16 [27, 96, 96], replicated, may hold values from -0.125 to 0.125
- w_down: bfloat16 [27, 192, 96], replicated, may hold values from -0.125 to 0.125
- cotangent: bfloat16 [8, 192, 32, 2, 128], P('rep', None, 'slab'), may hold values from -6 to 6
Outputs:
- section_out: bfloat16 [8, 192, 32, 2, 128], P('rep', None, 'slab')
- grad_features: bfloat16 [8, 96, 64, 4, 256], P('rep', None, 'slab')
- grad_fine: float32 [27, 96, 96], replicated
- grad_down: float32 [27, 192, 96], replicated
The draws below stay inside these ranges and needn't reach their ends.
Inputs may be any that keep to these rules, and one draw needn't show every extreme that they name: `occupancy`: 1 marks an occupied voxel; the share of occupied voxels differs from plane to plane.
All inputs are finite; a program needn't handle non-finite values.
Results may differ from the reference program's by a relative error of at most 0.0058.
Values may be sent and summed in bfloat16 or wider, within the bound.
A program may use at most 128 MiB of HBM per device.

```python
import jax
import jax.numpy as jnp
from jax import lax

C1 = 96
C2 = 192
NY = 4
NZ = 256
TILES = 8
NX = 64
CELLS = 65536


def draw_occupancy(key, part):
    key_plane = jax.random.fold_in(key, 11)
    key_voxel = jax.random.fold_in(key, 23)
    limits = jax.random.randint(key_plane, (TILES, NX, 1, 1), 15, 91)
    votes = jax.random.randint(key_voxel, (TILES, NX, NY, NZ), 0, 100)
    return (votes < limits).astype(jnp.int32)


def level_of(stream_key, extent, pieces, least, largest):
    level, own = 1.0, jax.random.fold_in(stream_key, 6)
    for axis_at, blocks in pieces:
        steps = jnp.exp(jax.random.uniform(jax.random.fold_in(own, axis_at), (blocks,), jnp.float32, least / len(pieces), largest / len(pieces)))
        level = level * jnp.repeat(steps, extent[axis_at] // blocks).reshape([-1 if axis == axis_at else 1 for axis in range(len(extent))])
    return level


def bell_draw(own_key, dims, spread, bound, shards=(), dtype=jnp.bfloat16):
    array = spread * jax.random.normal(own_key, dims, jnp.float32)
    if shards:
        array = array * level_of(own_key, dims, shards, -0.22, 0.18)
    return jnp.clip(array, -bound, bound).astype(dtype)


def setup_inputs(seed: int = 0) -> dict:
    key_of = jax.random.split(jax.random.key(seed), 6)
    return {
        "features": bell_draw(key_of[0], (TILES, C1, NX, NY, NZ), 1.0, 6.0, ((0, 8), (2, 32))),
        "occupancy": draw_occupancy(jax.random.fold_in(key_of[5], 71), 0),
        "w_fine": bell_draw(key_of[2], (27, C1, C1), (27 * C1) ** -0.5, 0.125),
        "w_down": bell_draw(key_of[3], (27, C2, C1), (27 * C1) ** -0.5, 0.125),
        "cotangent": bell_draw(key_of[4], (TILES, C2, NX // 2, NY // 2, NZ // 2), 1.0, 6.0, ((0, 8), (2, 32))),
    }


def dsilu(value):
    sig = jax.nn.sigmoid(value)
    return sig * (1.0 + value * (1.0 - sig))

def conv_same(padded, weights):
    planes = padded.shape[1] - 2
    rows = padded.shape[2] - 2
    cols = padded.shape[3] - 2
    total = jnp.zeros((weights.shape[1], planes, rows, cols), jnp.float32)
    for offset in range(27):
        dx, dy, dz = (offset // 9, offset // 3 % 3, offset % 3)
        piece = padded[:, dx:dx + planes, dy:dy + rows, dz:dz + cols]
        total = total + jnp.einsum('dc,cpyz->dpyz', weights[offset], piece)
    return total

def wgrad_same(grad, padded):
    planes, rows, cols = (grad.shape[1], grad.shape[2], grad.shape[3])
    parts = []
    for offset in range(27):
        dx, dy, dz = (offset // 9, offset // 3 % 3, offset % 3)
        piece = padded[:, dx:dx + planes, dy:dy + rows, dz:dz + cols]
        parts.append(jnp.einsum('dpyz,cpyz->dc', grad, piece))
    return jnp.stack(parts)

def conv_down(padded, weights):
    planes = (padded.shape[1] - 1) // 2
    rows = (padded.shape[2] - 1) // 2
    cols = (padded.shape[3] - 1) // 2
    total = jnp.zeros((weights.shape[1], planes, rows, cols), jnp.float32)
    for offset in range(27):
        dx, dy, dz = (offset // 9, offset // 3 % 3, offset % 3)
        piece = padded[:, dx:dx + 2 * planes:2, dy:dy + 2 * rows:2, dz:dz + 2 * cols:2]
        total = total + jnp.einsum('dc,cpyz->dpyz', weights[offset], piece)
    return total

def wgrad_down(grad, padded):
    planes, rows, cols = (grad.shape[1], grad.shape[2], grad.shape[3])
    parts = []
    for offset in range(27):
        dx, dy, dz = (offset // 9, offset // 3 % 3, offset % 3)
        piece = padded[:, dx:dx + 2 * planes:2, dy:dy + 2 * rows:2, dz:dz + 2 * cols:2]
        parts.append(jnp.einsum('dpyz,cpyz->dc', grad, piece))
    return jnp.stack(parts)

def back_down(grad, weights, planes_in):
    planes, rows, cols = (grad.shape[1], grad.shape[2], grad.shape[3])
    total = jnp.zeros((weights.shape[2], planes_in, 2 * rows + 1, 2 * cols + 1), jnp.float32)
    for offset in range(27):
        dx, dy, dz = (offset // 9, offset // 3 % 3, offset % 3)
        term = jnp.einsum('dc,dpyz->cpyz', weights[offset], grad)
        total = total.at[:, dx:dx + 2 * planes:2, dy:dy + 2 * rows:2, dz:dz + 2 * cols:2].add(term)
    return total

def one_tile(features, occupancy, cotangent, w_fine, w_down):
    mask = occupancy.astype(jnp.float32)
    masked = (features.astype(jnp.float32) * mask).astype(jnp.bfloat16)
    fine_pad = jnp.pad(masked.astype(jnp.float32), ((0, 0), (1, 1), (1, 1), (1, 1)))
    fine_pre = conv_same(fine_pad, w_fine)
    hidden = (jax.nn.silu(fine_pre) * mask).astype(jnp.bfloat16)
    size_x, size_y, size_z = mask.shape
    coarse_mask = mask.reshape(size_x // 2, 2, size_y // 2, 2, size_z // 2, 2).max(axis=(1, 3, 5))
    down_pad = jnp.pad(hidden.astype(jnp.float32), ((0, 0), (1, 0), (1, 0), (1, 0)))
    down_pre = conv_down(down_pad, w_down)
    section_out = (jax.nn.silu(down_pre) * coarse_mask).astype(jnp.bfloat16)
    grad_pre = (cotangent.astype(jnp.float32) * coarse_mask * dsilu(down_pre)).astype(jnp.bfloat16)
    grad_pre32 = grad_pre.astype(jnp.float32)
    grad_down = wgrad_down(grad_pre32, down_pad)
    grad_hidden = back_down(grad_pre32, w_down, size_x + 1)[:, 1:, 1:, 1:]
    grad_fine_pre = (grad_hidden * mask * dsilu(fine_pre)).astype(jnp.bfloat16)
    gfp32 = grad_fine_pre.astype(jnp.float32)
    grad_fine = wgrad_same(gfp32, fine_pad)
    flipped = jnp.transpose(w_fine[::-1], (0, 2, 1))
    back_pad = jnp.pad(gfp32, ((0, 0), (1, 1), (1, 1), (1, 1)))
    grad_features = (conv_same(back_pad, flipped) * mask).astype(jnp.bfloat16)
    return (section_out, grad_features, grad_fine, grad_down)

def reference(features, occupancy, w_fine, w_down, cotangent):
    fine32 = w_fine.astype(jnp.float32)
    down32 = w_down.astype(jnp.float32)

    def tile_fn(items):
        return one_tile(items[0], items[1], items[2], fine32, down32)
    section_out, grad_features, fine_parts, down_parts = lax.map(tile_fn, (features, occupancy, cotangent))
    scale = 1.0 / jnp.sqrt(jnp.float32(CELLS))
    grad_fine = lax.optimization_barrier(jnp.sum(fine_parts, axis=0)) * scale
    grad_down = lax.optimization_barrier(jnp.sum(down_parts, axis=0)) * scale
    return (section_out, grad_features, grad_fine, grad_down)
```

```python
import jax
import jax.numpy as jnp
from jax import lax
from jax.experimental import pallas as pl
from jax.experimental.pallas import tpu as pltpu
from jax.sharding import PartitionSpec as P

BF = jnp.bfloat16
F32 = jnp.float32
NT = (((1,), (1,)), ((), ()))
HD = 176
HF = 96


def mm(a, b):
    return jnp.dot(a, b, preferred_element_type=F32)


def mm_nt(a, b):
    return lax.dot_general(a, b, NT, preferred_element_type=F32)


def lane_ids(shape):
    return lax.broadcasted_iota(jnp.int32, shape, 1)


def from_before(v):
    return jnp.where(lane_ids(v.shape) == 0, 0.0, pltpu.roll(v, 1, 1))


def from_after(v):
    n = v.shape[1]
    return jnp.where(lane_ids(v.shape) == n - 1, 0.0, pltpu.roll(v, n - 1, 1))


def split_z(n):
    r = lax.broadcasted_iota(jnp.int32, (n, n), 0)
    c = lax.broadcasted_iota(jnp.int32, (n, n), 1)
    src = jnp.where(c < n // 2, 2 * c, 2 * c - n + 1)
    return (r == src).astype(F32).astype(BF)


def join_z(n):
    r = lax.broadcasted_iota(jnp.int32, (n, n), 0)
    c = lax.broadcasted_iota(jnp.int32, (n, n), 1)
    src = jnp.where(r < n // 2, 2 * r, 2 * r - n + 1)
    return (c == src).astype(F32).astype(BF)


def gather_dz(acc, c):
    a0, a1, a2 = acc[:c], acc[c : 2 * c], acc[2 * c :]
    even = from_before(a0[:, 128:]) + a1[:, :128] + a2[:, 128:]
    odd = a0[:, :128] + a1[:, 128:] + from_after(a2[:, :128])
    return jnp.concatenate([even, odd], axis=1)


class Place:
    def __init__(self):
        self.slab = lax.axis_index("slab")
        self.rep = lax.axis_index("rep")
        self.core = self.slab % 2
        self.x = (self.slab // 2) % 4
        self.zlo = self.slab // 8
        self.y = self.rep % 4
        self.zhi = self.rep // 4
        self.z = self.zhi * 4 + self.zlo

    def at(self, core, x, y, z):
        return {"slab": (z % 4) * 8 + x * 2 + core, "rep": (z // 4) * 4 + y}

    def partner(self):
        return self.at(1 - self.core, self.x, self.y, self.z)

    def plane(self, k, sign=1):
        x = (self.x + sign * (k // 4) + 4) % 4
        y = (self.y + sign * (k % 4) + 4) % 4
        return x, y

    def plane_dev(self, k):
        x, y = self.plane(k)
        return self.at(self.core, x, y, self.z)

    def z_dev(self, k):
        return self.at(self.core, self.x, self.y, (self.z + k) % 8)


def remote(src, dst, ssem, rsem, dev):
    return pltpu.make_async_remote_copy(
        src_ref=src, dst_ref=dst, send_sem=ssem, recv_sem=rsem, device_id=dev,
        device_id_type=pl.DeviceIdType.MESH,
    )


class Sum:
    def __init__(self, at, h, part, out, cbuf, acc, rs, zb, sems):
        self.at, self.h = at, h
        self.part, self.out, self.cbuf, self.acc, self.rs, self.zb = part, out, cbuf, acc, rs, zb
        self.ss, self.rr = sems
        self.sent = []

    def rows(self, start):
        return pl.ds(pl.multiple_of(start, 16), self.h)

    def copy(self, src, dst, i, dev):
        c = remote(src, dst, self.ss.at[i], self.rr.at[i], dev)
        c.start()
        self.sent.append(c)
        return c

    def half(self, core):
        return pl.ds(pl.multiple_of(core * (16 * self.h), 16), 16 * self.h)

    def one(self):
        self.c1 = self.copy(self.part.at[self.half(1 - self.at.core)], self.cbuf, 0, self.at.partner())

    def two(self):
        self.c1.wait_recv()
        h, at = self.h, self.at
        self.c2 = []
        for k in list(range(1, 16)) + [0]:
            x, y = at.plane(k)
            m = x * 4 + y
            mine = self.part[self.rows(at.core * (16 * h) + m * h), :].astype(F32)
            both = mine + self.cbuf[self.rows(m * h), :].astype(F32)
            self.acc[self.rows(m * h), :] = both.astype(BF)
            if k:
                self.c2.append(self.copy(self.acc.at[self.rows(m * h)], self.rs.at[k], k, at.plane_dev(k)))

    def three(self):
        h, at = self.h, self.at
        total = self.acc[self.rows((at.x * 4 + at.y) * h), :].astype(F32)
        for k in range(1, 16):
            self.c2[k - 1].wait_recv()
            total = total + self.rs[k].astype(F32)
        self.zb[at.z] = total.astype(BF)
        self.c3 = [
            self.copy(self.zb.at[at.z], self.zb.at[at.z], 16 + k, at.z_dev(k)) for k in range(1, 8)
        ]

    def four(self):
        h, at = self.h, self.at
        for c in self.c3:
            c.wait_recv()
        total = self.zb[0].astype(F32)
        for k in range(1, 8):
            total = total + self.zb[k].astype(F32)
        mine = self.rows(at.core * (16 * h) + (at.x * 4 + at.y) * h)
        self.out[mine, :] = total.astype(BF)
        self.c4 = [
            self.copy(self.out.at[mine], self.out.at[mine], 24 + k, at.plane_dev(k)) for k in range(1, 16)
        ]
        self.c5 = [self.copy(self.out.at[mine], self.out.at[mine], 40, at.partner())]

    def five(self):
        h, at = self.h, self.at
        for k in range(1, 16):
            self.c4[k - 1].wait_recv()
            x, y = at.plane(k, -1)
            rows = self.rows(at.core * (16 * h) + (x * 4 + y) * h)
            self.c5.append(self.copy(self.out.at[rows], self.out.at[rows], 40 + k, at.partner()))

    def six(self):
        for c in self.c5:
            c.wait_recv()
        for c in self.sent:
            c.wait_send()


def kernel(
    xm, occ, wf, wft, wd, wdt, cot,
    gf, so, dout, fout,
    xb, gb, hb, hs, ds, kf, kb, kd, gs, gp, gn, raw,
    dpart, dcb, dacc, drs, dzb, fpart, fcb, facc, frs, fzb,
    hs_s, hs_r, dsem_s, dsem_r, fsem_s, fsem_r,
):
    at = Place()
    first, last = at.slab == 0, at.slab == 31
    left = {"slab": jnp.maximum(at.slab - 1, 0), "rep": at.rep}
    right = {"slab": jnp.minimum(at.slab + 1, 31), "rep": at.rep}
    barrier = pltpu.get_barrier_semaphore()

    def greet(dev):
        pl.semaphore_signal(barrier, 1, device_id=dev, device_id_type=pl.DeviceIdType.MESH)

    @pl.when(jnp.logical_not(first))
    def _():
        greet(left)

    @pl.when(jnp.logical_not(last))
    def _():
        greet(right)

    for k in range(1, 16):
        greet(at.plane_dev(k))
    for k in range(1, 8):
        greet(at.z_dev(k))

    kf[...] = jnp.zeros_like(kf)
    kb[...] = jnp.zeros_like(kb)
    kd[...] = jnp.zeros_like(kd)
    for j in range(9):
        kf[:, 128 * j : 128 * j + 96] = wf[3 * j : 3 * j + 3].reshape(288, 96)
        kb[:, 128 * j : 128 * j + 96] = wft[3 * j : 3 * j + 3].reshape(288, 96)
    for o in range(27):
        kd[:, 128 * o : 128 * o + 96] = wd[o]

    pz = split_z(256)
    for b in (xb, gb):
        for p in range(4):
            b[p, 0] = jnp.zeros((128, 256), BF)
            b[p, 5] = jnp.zeros((128, 256), BF)
            for q in range(1, 5):
                b[p, q, 96:] = jnp.zeros((32, 256), BF)
    for p in range(3):
        hb[p, 0] = jnp.zeros((96, 256), BF)
    for o in range(27):
        hs[128 * o + 96 : 128 * o + 128, :] = jnp.zeros((32, 256), BF)

    amount = 22 + jnp.where(first, 0, 1) + jnp.where(last, 0, 1)
    pl.semaphore_wait(barrier, amount)

    def exchange(src_l, dst_l, src_r, dst_r, i, zero_l, zero_r):
        cl = remote(src_l, dst_l, hs_s.at[i], hs_r.at[i], left) if src_l is not None else None
        cr = remote(src_r, dst_r, hs_s.at[i + 1], hs_r.at[i + 1], right) if src_r is not None else None

        def start():
            if cl is not None:
                @pl.when(jnp.logical_not(first))
                def _():
                    cl.start()
            if cr is not None:
                @pl.when(jnp.logical_not(last))
                def _():
                    cr.start()

        def arrive():
            if cl is not None:
                @pl.when(jnp.logical_not(last))
                def _():
                    cl.wait_recv()

                @pl.when(last)
                def _():
                    zero_l()
            if cr is not None:
                @pl.when(jnp.logical_not(first))
                def _():
                    cr.wait_recv()

                @pl.when(first)
                def _():
                    zero_r()

        def done():
            if cl is not None:
                @pl.when(jnp.logical_not(first))
                def _():
                    cl.wait_send()
            if cr is not None:
                @pl.when(jnp.logical_not(last))
                def _():
                    cr.wait_send()

        return start, arrive, done

    def fill(ref):
        def f():
            ref[...] = jnp.zeros(ref.shape, BF)
        return f

    a_start, a_arrive, a_done = exchange(
        xm.at[0], raw.at[1], xm.at[1], raw.at[0], 0, fill(raw.at[1]), fill(raw.at[0])
    )
    a_start()
    masks = []
    for p in range(2):
        masks.append(mm(occ[p].astype(F32).astype(BF), pz))
    mask = lambda p, q: masks[p][q : q + 1]
    for p in range(2):
        for q in range(4):
            xb[1 + p, 1 + q, :96] = mm(xm[p, q], pz).astype(BF)
    a_arrive()
    for p in range(2):
        for q in range(4):
            xb[3 * p, 1 + q, :96] = mm(raw[p, q], pz).astype(BF)

    b_start, b_arrive, b_done = exchange(
        None, None, hb.at[2, pl.ds(1, 4)], hb.at[0, pl.ds(1, 4)], 2, None, fill(hb.at[0, pl.ds(1, 4)])
    )

    def conv(weights, b, p, q):
        stack = jnp.concatenate([b[p + dx, q + dy] for dx in range(3) for dy in range(3)], axis=0)
        return gather_dz(mm(weights[...], stack), 96)

    for p in (1, 0):
        for q in range(4):
            pre = conv(kf, xb, p, q)
            sig = jax.nn.sigmoid(pre)
            hb[1 + p, 1 + q] = (pre * sig * mask(p, q)).astype(BF)
            ds[p, q] = mask(p, q) * (sig * (1.0 + pre * (1.0 - sig)))
        if p == 1:
            b_start()

    def fill_hs(dx):
        for dy in range(3):
            for j in range(2):
                v = hb[dx, 2 * j + dy]
                lanes = slice(128 * j, 128 * j + 128)
                base = 128 * (9 * dx + 3 * dy)
                hs[base : base + 96, lanes] = from_before(v[:, 128:].astype(F32)).astype(BF)
                hs[base + 128 : base + 224, lanes] = v[:, :128]
                hs[base + 256 : base + 352, lanes] = v[:, 128:]

    fill_hs(1)
    fill_hs(2)
    b_arrive()
    fill_hs(0)
    down = mm(kd[...], hs[...])
    coarse = []
    for j in range(2):
        m = [mask(p, 2 * j + q) for p in range(2) for q in range(2)]
        m = jnp.maximum(jnp.maximum(m[0], m[1]), jnp.maximum(m[2], m[3]))
        coarse.append(jnp.maximum(m[:, :128], m[:, 128:]))
    cm = jnp.concatenate(coarse, axis=1)
    sig = jax.nn.sigmoid(down)
    so[...] = (down * sig * cm).astype(BF)
    gp[...] = (cot[...].astype(F32) * cm * (sig * (1.0 + down * (1.0 - sig)))).astype(BF)
    c_start, c_arrive, c_done = exchange(gp, gn, None, None, 4, fill(gn), None)
    c_start()

    dsum = Sum(at, HD, dpart, dout, dcb, dacc, drs, dzb, (dsem_s, dsem_r))
    fsum = Sum(at, HF, fpart, fout, fcb, facc, frs, fzb, (fsem_s, fsem_r))
    for o in range(27):
        dpart[192 * o : 192 * o + 192, :] = mm_nt(gp[...], hs[128 * o : 128 * o + 128, :]).astype(BF)
    dpart[27 * 192 :, :] = jnp.zeros((32 * HD - 27 * 192, 128), BF)
    dsum.one()

    def back(dx, g):
        r = mm(wdt[9 * dx : 9 * dx + 9].reshape(864, 192), g[...])
        out = []
        for q, terms in enumerate((((0, 1),), ((0, 2), (1, 0)), ((1, 1),), ((1, 2),))):
            even, odd = 0.0, 0.0
            for j, dy in terms:
                lanes = slice(128 * j, 128 * j + 128)
                r0, r1, r2 = [r[96 * (3 * dy + dz) : 96 * (3 * dy + dz) + 96, lanes] for dz in range(3)]
                even = even + r1
                odd = odd + r2 + from_after(r0)
            out.append(jnp.concatenate([even, odd], axis=1))
        return out

    for q, v in enumerate(back(1, gp)):
        gb[1, 1 + q, :96] = (v * ds[0, q]).astype(BF)
    own = back(2, gp)
    c_arrive()
    nxt = back(0, gn)
    for q in range(4):
        gb[2, 1 + q, :96] = ((own[q] + nxt[q]) * ds[1, q]).astype(BF)
    inner = (pl.ds(1, 4), pl.ds(0, 96))
    d_start, d_arrive, d_done = exchange(
        gb.at[(1,) + inner], gb.at[(3,) + inner], gb.at[(2,) + inner], gb.at[(0,) + inner], 6,
        fill(gb.at[(3,) + inner]), fill(gb.at[(0,) + inner]),
    )
    d_start()
    dsum.two()

    for p in range(2):
        for q in range(4):
            g = gb[1 + p, 1 + q, :96].astype(F32)
            ge, go = g[:, :128], g[:, 128:]
            base = 256 * (4 * p + q)
            gs[0:96, base : base + 128] = go.astype(BF)
            gs[0:96, base + 128 : base + 256] = from_after(ge).astype(BF)
            gs[96:192, base : base + 256] = g.astype(BF)
            gs[192:288, base : base + 128] = from_before(go).astype(BF)
            gs[192:288, base + 128 : base + 256] = ge.astype(BF)
    for j0 in range(0, 9, 2):
        js = [j for j in (j0, j0 + 1) if j < 9]
        rhs = jnp.concatenate(
            [
                jnp.concatenate([xb[p + j // 3, q + j % 3] for p in range(2) for q in range(4)], axis=1)
                for j in js
            ],
            axis=0,
        )
        r = mm_nt(gs[...], rhs)
        for i, j in enumerate(js):
            fpart[288 * j : 288 * j + 288, :] = r[:, 128 * i : 128 * i + 128].astype(BF)
    fpart[27 * 96 :, :] = jnp.zeros((32 * HF - 27 * 96, 128), BF)
    fsum.one()
    dsum.three()
    fsum.two()
    d_arrive()

    jz = join_z(256)
    for p in range(2):
        for q in range(4):
            g = (conv(kb, gb, p, q) * mask(p, q)).astype(BF)
            gf[p, q] = mm(g, jz).astype(BF)
    dsum.four()
    fsum.three()
    dsum.five()
    fsum.four()
    fsum.five()
    dsum.six()
    fsum.six()
    a_done()
    b_done()
    c_done()
    d_done()


def local(features, occupancy, w_fine, w_down, cotangent):
    mask = occupancy[0].astype(F32)
    masked = (features[0] * mask).astype(BF)
    xm = jnp.transpose(masked, (1, 2, 0, 3))
    wft = jnp.transpose(w_fine[::-1], (0, 2, 1))
    wdt = jnp.transpose(w_down, (0, 2, 1))
    cot = cotangent[0].reshape(192, 256)
    vm = pl.BlockSpec(memory_space=pltpu.VMEM)

    def sums(h):
        return [
            pltpu.VMEM((32 * h, 128), BF), pltpu.VMEM((16 * h, 128), BF), pltpu.VMEM((16 * h, 128), BF),
            pltpu.VMEM((16, h, 128), BF), pltpu.VMEM((8, h, 128), BF),
        ]

    dma = pltpu.SemaphoreType.DMA
    gf, so, dout, fout = pl.pallas_call(
        kernel,
        out_shape=(
            jax.ShapeDtypeStruct((2, 4, 96, 256), BF),
            jax.ShapeDtypeStruct((192, 256), BF),
            jax.ShapeDtypeStruct((32 * HD, 128), BF),
            jax.ShapeDtypeStruct((32 * HF, 128), BF),
        ),
        in_specs=[vm] * 7,
        out_specs=(vm,) * 4,
        scratch_shapes=[
            pltpu.VMEM((4, 6, 128, 256), BF),
            pltpu.VMEM((4, 6, 128, 256), BF),
            pltpu.VMEM((3, 5, 96, 256), BF),
            pltpu.VMEM((27 * 128, 256), BF),
            pltpu.VMEM((2, 4, 96, 256), F32),
            pltpu.VMEM((288, 1152), BF),
            pltpu.VMEM((288, 1152), BF),
            pltpu.VMEM((192, 27 * 128), BF),
            pltpu.VMEM((288, 2048), BF),
            pltpu.VMEM((192, 256), BF),
            pltpu.VMEM((192, 256), BF),
            pltpu.VMEM((2, 4, 96, 256), BF),
        ]
        + sums(HD)
        + sums(HF)
        + [dma((8,)), dma((8,)), dma((56,)), dma((56,)), dma((56,)), dma((56,))],
        compiler_params=pltpu.CompilerParams(
            collective_id=0, has_side_effects=True, vmem_limit_bytes=60 * 2**20
        ),
        name="section",
    )(xm, occupancy[0], w_fine, wft, w_down, wdt, cot)
    scale = 1.0 / jnp.sqrt(jnp.float32(65536))
    total_down = dout[: 27 * 192].reshape(27, 192, 128)[:, :, :96].astype(F32) * scale
    total_fine = fout[: 27 * 96].reshape(27, 96, 128)[:, :, :96].astype(F32) * scale
    return (
        so.reshape(1, 192, 1, 2, 128),
        jnp.transpose(gf, (2, 0, 1, 3))[None],
        total_fine,
        total_down,
    )


def solution(mesh):
    return jax.shard_map(
        local,
        mesh=mesh,
        in_specs=(
            P("rep", None, "slab", None, None),
            P("rep", "slab", None, None),
            P(),
            P(),
            P("rep", None, "slab", None, None),
        ),
        out_specs=(
            P("rep", None, "slab", None, None),
            P("rep", None, "slab", None, None),
            P(),
            P(),
        ),
        check_vma=False,
    )
```

```python
import jax
import jax.numpy as jnp
from jax import lax
from jax.experimental import pallas as pl
from jax.experimental.pallas import tpu as pltpu
from jax.sharding import PartitionSpec as P

BF = jnp.bfloat16
F32 = jnp.float32
NT = (((1,), (1,)), ((), ()))
HD = 128
HF = 64


def mm(a, b):
    return jnp.dot(a, b, preferred_element_type=F32)


def mm_nt(a, b):
    return lax.dot_general(a, b, NT, preferred_element_type=F32)


def lane_ids(shape):
    return lax.broadcasted_iota(jnp.int32, shape, 1)


def from_before(v):
    return jnp.where(lane_ids(v.shape) == 0, 0.0, pltpu.roll(v, 1, 1))


def from_after(v):
    n = v.shape[1]
    return jnp.where(lane_ids(v.shape) == n - 1, 0.0, pltpu.roll(v, n - 1, 1))


def split_z(n):
    r = lax.broadcasted_iota(jnp.int32, (n, n), 0)
    c = lax.broadcasted_iota(jnp.int32, (n, n), 1)
    src = jnp.where(c < n // 2, 2 * c, 2 * c - n + 1)
    return (r == src).astype(F32).astype(BF)


def join_z(n):
    r = lax.broadcasted_iota(jnp.int32, (n, n), 0)
    c = lax.broadcasted_iota(jnp.int32, (n, n), 1)
    src = jnp.where(r < n // 2, 2 * r, 2 * r - n + 1)
    return (c == src).astype(F32).astype(BF)


def gather_dz(acc, c):
    a0, a1, a2 = acc[:c], acc[c : 2 * c], acc[2 * c :]
    even = from_before(a0[:, 128:]) + a1[:, :128] + a2[:, 128:]
    odd = a0[:, :128] + a1[:, 128:] + from_after(a2[:, :128])
    return jnp.concatenate([even, odd], axis=1)


class Place:
    def __init__(self):
        self.slab = lax.axis_index("slab")
        self.rep = lax.axis_index("rep")
        self.core = self.slab % 2
        self.x = (self.slab // 2) % 4
        self.zlo = self.slab // 8
        self.y = self.rep % 4
        self.zhi = self.rep // 4
        self.z = self.zhi * 4 + self.zlo

    def at(self, core, x, y, z):
        return {"slab": (z % 4) * 8 + x * 2 + core, "rep": (z // 4) * 4 + y}

    def partner(self):
        return self.at(1 - self.core, self.x, self.y, self.z)

    def plane(self, k, sign=1):
        x = (self.x + sign * (k // 4) + 4) % 4
        y = (self.y + sign * (k % 4) + 4) % 4
        return x, y

    def plane_dev(self, k):
        x, y = self.plane(k)
        return self.at(self.core, x, y, self.z)

    def z_dev(self, k):
        return self.at(self.core, self.x, self.y, (self.z + k) % 8)


def remote(src, dst, ssem, rsem, dev):
    return pltpu.make_async_remote_copy(
        src_ref=src, dst_ref=dst, send_sem=ssem, recv_sem=rsem, device_id=dev,
        device_id_type=pl.DeviceIdType.MESH,
    )


class Sum:
    def __init__(self, at, h, part, out, cbuf, acc, rs, zb, sems):
        self.at, self.h = at, h
        self.part, self.out, self.cbuf, self.acc, self.rs, self.zb = part, out, cbuf, acc, rs, zb
        self.ss, self.rr = sems
        self.sent = []

    def rows(self, start):
        return pl.ds(pl.multiple_of(start, 16), self.h)

    def copy(self, src, dst, i, dev):
        c = remote(src, dst, self.ss.at[i], self.rr.at[i], dev)
        c.start()
        self.sent.append(c)
        return c

    def half(self, core):
        return pl.ds(pl.multiple_of(core * (16 * self.h), 16), 16 * self.h)

    def one(self):
        self.c1 = self.copy(self.part.at[self.half(1 - self.at.core)], self.cbuf, 0, self.at.partner())

    def two(self):
        self.c1.wait_recv()
        h, at = self.h, self.at
        self.c2 = []
        for k in list(range(1, 16)) + [0]:
            x, y = at.plane(k)
            m = x * 4 + y
            mine = self.part[self.rows(at.core * (16 * h) + m * h), :].astype(F32)
            both = mine + self.cbuf[self.rows(m * h), :].astype(F32)
            self.acc[self.rows(m * h), :] = both.astype(BF)
            if k:
                self.c2.append(self.copy(self.acc.at[self.rows(m * h)], self.rs.at[k], k, at.plane_dev(k)))

    def three(self):
        h, at = self.h, self.at
        total = self.acc[self.rows((at.x * 4 + at.y) * h), :].astype(F32)
        for k in range(1, 16):
            self.c2[k - 1].wait_recv()
            total = total + self.rs[k].astype(F32)
        self.zb[at.z] = total.astype(BF)
        self.c3 = [
            self.copy(self.zb.at[at.z], self.zb.at[at.z], 16 + k, at.z_dev(k)) for k in range(1, 8)
        ]

    def four(self):
        h, at = self.h, self.at
        for c in self.c3:
            c.wait_recv()
        total = self.zb[0].astype(F32)
        for k in range(1, 8):
            total = total + self.zb[k].astype(F32)
        mine = self.rows(at.core * (16 * h) + (at.x * 4 + at.y) * h)
        self.out[mine, :] = total.astype(BF)
        self.c4 = [
            self.copy(self.out.at[mine], self.out.at[mine], 24 + k, at.plane_dev(k)) for k in range(1, 16)
        ]
        self.c5 = [self.copy(self.out.at[mine], self.out.at[mine], 40, at.partner())]

    def five(self):
        h, at = self.h, self.at
        for k in range(1, 16):
            self.c4[k - 1].wait_recv()
            x, y = at.plane(k, -1)
            rows = self.rows(at.core * (16 * h) + (x * 4 + y) * h)
            self.c5.append(self.copy(self.out.at[rows], self.out.at[rows], 40 + k, at.partner()))

    def six(self):
        for c in self.c5:
            c.wait_recv()
        for c in self.sent:
            c.wait_send()


def packed(ref, rows, tile, slot):
    tile, off = tile + 96 * slot // 128, 96 * slot % 128
    a = ref[rows * tile : rows * tile + rows, :]
    if off == 0:
        return a[:, :96]
    if off == 32:
        return a[:, 32:]
    b = ref[rows * (tile + 1) : rows * (tile + 1) + rows, :]
    return jnp.concatenate([a[:, off:], b[:, : off - 32]], axis=1)


def put_tiles(ref, rows, tile, v):
    extra = -v.shape[1] % 128
    if extra:
        v = jnp.concatenate([v, jnp.zeros((rows, extra), v.dtype)], axis=1)
    for i in range(v.shape[1] // 128):
        ref[rows * (tile + i) : rows * (tile + i) + rows, :] = v[:, 128 * i : 128 * i + 128].astype(BF)


def kernel(
    xm, occ, wf, wd, cot,
    gf, so, dout, fout,
    xb, gb, hs, ds, part, kf, kb, kd, kt, gs, gp, gn, bp, bn, raw,
    dpart, dfull, dcb, dacc, drs, dzb, fpart, ffull, fcb, facc, frs, fzb,
    hs_s, hs_r, dsem_s, dsem_r, fsem_s, fsem_r,
):
    at = Place()
    first, last = at.slab == 0, at.slab == 31
    left = {"slab": jnp.maximum(at.slab - 1, 0), "rep": at.rep}
    right = {"slab": jnp.minimum(at.slab + 1, 31), "rep": at.rep}
    barrier = pltpu.get_barrier_semaphore()

    def greet(dev):
        pl.semaphore_signal(barrier, 1, device_id=dev, device_id_type=pl.DeviceIdType.MESH)

    @pl.when(jnp.logical_not(first))
    def _():
        greet(left)

    @pl.when(jnp.logical_not(last))
    def _():
        greet(right)

    for k in range(1, 16):
        greet(at.plane_dev(k))
    for k in range(1, 8):
        greet(at.z_dev(k))

    class Edge:
        def __init__(self, i, to_left=None, to_right=None):
            self.l = self.r = None
            if to_left is not None:
                self.l = remote(*to_left, hs_s.at[i], hs_r.at[i], left)
                self.lz = to_left[1]
            if to_right is not None:
                self.r = remote(*to_right, hs_s.at[i + 1], hs_r.at[i + 1], right)
                self.rz = to_right[1]

        def start(self):
            if self.l is not None:
                pl.when(jnp.logical_not(first))(self.l.start)
            if self.r is not None:
                pl.when(jnp.logical_not(last))(self.r.start)

        def from_right(self):
            pl.when(jnp.logical_not(last))(self.l.wait_recv)

            @pl.when(last)
            def _():
                self.lz[...] = jnp.zeros(self.lz.shape, BF)

        def from_left(self):
            pl.when(jnp.logical_not(first))(self.r.wait_recv)

            @pl.when(first)
            def _():
                self.rz[...] = jnp.zeros(self.rz.shape, BF)

        def done(self):
            if self.l is not None:
                pl.when(jnp.logical_not(first))(self.l.wait_send)
            if self.r is not None:
                pl.when(jnp.logical_not(last))(self.r.wait_send)

    inner = (pl.ds(1, 4), slice(None))
    edge_x = Edge(0, (xm.at[0], raw.at[1]), (xm.at[1], raw.at[0]))
    edge_b = Edge(2, to_right=(bp, bn))
    edge_g = Edge(4, to_left=(gp, gn))
    edge_d = Edge(6, (gb.at[(1,) + inner], gb.at[(3,) + inner]), (gb.at[(2,) + inner], gb.at[(0,) + inner]))

    pz = split_z(256)
    masks = [mm(occ[p].astype(F32).astype(BF), pz) for p in range(2)]
    mask = lambda p, q: masks[p][q : q + 1]
    for p in range(2):
        for q in range(4):
            xb[1 + p, 1 + q] = mm(xm[p, q], pz).astype(BF)
    for b in (xb, gb):
        for p in range(4):
            b[p, 0] = jnp.zeros((96, 256), BF)
            b[p, 5] = jnp.zeros((96, 256), BF)
    for dx in range(3):
        for dy in range(3):
            base = 384 * dx + 96 * dy
            kf[:, base : base + 96] = wf[9 * dx + 3 * dy : 9 * dx + 3 * dy + 3].reshape(288, 96)
        kf[:, 384 * dx + 288 : 384 * dx + 384] = jnp.zeros((288, 96), BF)

    pl.semaphore_wait(barrier, 22 + jnp.where(first, 0, 1) + jnp.where(last, 0, 1))
    edge_x.start()

    gap = jnp.zeros((96, 256), BF)

    def rows_of(b, p, q):
        return [b[p, q + dy] for dy in range(3)]

    for p in range(2):
        for q in range(4):
            stack = jnp.concatenate(rows_of(xb, 1, q) + [gap] + rows_of(xb, 2, q), axis=0)
            base = 384 * (1 - p)
            part[p, q] = mm(kf[:, base : base + 672], stack)

    eye = (lax.broadcasted_iota(jnp.int32, (96, 96), 0) == lax.broadcasted_iota(jnp.int32, (96, 96), 1))
    eye = eye.astype(F32).astype(BF)
    for o in range(27):
        kd[o // 9, :, 96 * (o % 9) : 96 * (o % 9) + 96] = wd[o]
        kt[o] = mm_nt(eye, wd[o]).astype(BF)
        kb[96 * (o % 3) : 96 * (o % 3) + 96, 96 * (o // 3) : 96 * (o // 3) + 96] = mm_nt(eye, wf[26 - o]).astype(BF)

    def finish(p):
        for q in range(4):
            xb[3 * p, 1 + q] = mm(raw[p, q], pz).astype(BF)
        for q in range(4):
            base = 768 * p
            halo = mm(kf[:, base : base + 288], jnp.concatenate(rows_of(xb, 3 * p, q), axis=0))
            pre = gather_dz(part[p, q] + halo, 96)
            sig = jax.nn.sigmoid(pre)
            h = (pre * sig * mask(p, q)).astype(BF).astype(F32)
            ds[p, q] = mask(p, q) * (sig * (1.0 + pre * (1.0 - sig)))
            even, odd = h[:, :128].astype(BF), h[:, 128:].astype(BF)
            before = from_before(h[:, 128:]).astype(BF)
            for dy in range(3):
                if (q + 1 - dy) % 2 == 0 and 0 <= (q + 1 - dy) // 2 < 2:
                    j = (q + 1 - dy) // 2
                    lanes = slice(128 * j, 128 * j + 128)
                    for dz, v in enumerate((before, even, odd)):
                        row = 96 * (9 * p + 3 * dy + dz)
                        hs[row : row + 96, lanes] = v

    hs_zero = jnp.zeros((288, 128), BF)
    for p in range(2):
        hs[864 * p : 864 * p + 288, :128] = hs_zero
    edge_x.from_right()
    finish(1)
    bp[...] = mm(kd[0], hs[864:1728, :]).astype(BF)
    edge_b.start()
    edge_x.from_left()
    finish(0)
    down = mm(kd[1], hs[:864, :]) + mm(kd[2], hs[864:1728, :])
    order = join_z(384)
    cots = mm(order, cot[...])
    cots = jnp.concatenate([cots[:192], cots[192:]], axis=1)
    coarse = []
    for j in range(2):
        m = [mask(p, 2 * j + q) for p in range(2) for q in range(2)]
        m = jnp.maximum(jnp.maximum(m[0], m[1]), jnp.maximum(m[2], m[3]))
        coarse.append(jnp.maximum(m[:, :128], m[:, 128:]))
    cm = jnp.concatenate(coarse, axis=1)
    edge_b.from_left()
    down = down + bn[...].astype(F32)
    sig = jax.nn.sigmoid(down)
    gp[...] = (cots * cm * (sig * (1.0 + down * (1.0 - sig)))).astype(BF)
    edge_g.start()
    out = (down * sig * cm).astype(BF)
    out = jnp.concatenate([out[:, :128], out[:, 128:]], axis=0)
    so[...] = mm(split_z(384), out).astype(BF)

    dsum = Sum(at, HD, dpart, dfull, dcb, dacc, drs, dzb, (dsem_s, dsem_r))
    fsum = Sum(at, HF, fpart, ffull, fcb, facc, frs, fzb, (fsem_s, fsem_r))
    for n in range(0, 1728, 768):
        put_tiles(dpart, 192, n // 128, mm_nt(gp[...], hs[n : min(n + 768, 1728), :]))
    dpart[21 * 192 :, :] = jnp.zeros((32 * HD - 21 * 192, 128), BF)

    def back(dx, g):
        r = mm(kt[9 * dx : 9 * dx + 9].reshape(864, 192), g[...])
        out = []
        for q, terms in enumerate((((0, 1),), ((0, 2), (1, 0)), ((1, 1),), ((1, 2),))):
            even, odd = 0.0, 0.0
            for j, dy in terms:
                lanes = slice(128 * j, 128 * j + 128)
                r0, r1, r2 = [r[96 * (3 * dy + dz) : 96 * (3 * dy + dz) + 96, lanes] for dz in range(3)]
                even = even + r1
                odd = odd + r2 + from_after(r0)
            out.append(jnp.concatenate([even, odd], axis=1))
        return out

    for q, v in enumerate(back(1, gp)):
        gb[1, 1 + q] = (v * ds[0, q]).astype(BF)
    own = back(2, gp)
    edge_g.from_right()
    for n in range(0, 864, 768):
        put_tiles(dpart, 192, 14 + n // 128, mm_nt(gn[...], hs[864 + n : 864 + min(n + 768, 864), :]))
    dsum.one()
    nxt = back(0, gn)
    for q in range(4):
        gb[2, 1 + q] = ((own[q] + nxt[q]) * ds[1, q]).astype(BF)
    edge_d.start()

    for p in range(2):
        for q in range(4):
            g = gb[1 + p, 1 + q].astype(F32)
            ge, go = g[:, :128], g[:, 128:]
            base = 256 * (4 * p + q)
            gs[0:96, base : base + 128] = go.astype(BF)
            gs[0:96, base + 128 : base + 256] = from_after(ge).astype(BF)
            gs[96:192, base : base + 256] = g.astype(BF)
            gs[192:288, base : base + 128] = from_before(go).astype(BF)
            gs[192:288, base + 128 : base + 256] = ge.astype(BF)
    dsum.two()
    for j0 in range(0, 9, 4):
        rhs = jnp.concatenate(
            [
                jnp.concatenate([xb[p + j // 3, q + j % 3] for p in range(2) for q in range(4)], axis=1)
                for j in range(j0, min(j0 + 4, 9))
            ],
            axis=0,
        )
        put_tiles(fpart, 288, 3 * (j0 // 4), mm_nt(gs[...], rhs))
    fpart[7 * 288 :, :] = jnp.zeros((32 * HF - 7 * 288, 128), BF)
    fsum.one()
    edge_d.from_right()
    edge_d.from_left()

    jz = join_z(256)

    def grad_plane(p):
        for q in range(4):
            stack = jnp.concatenate([r for dx in range(3) for r in rows_of(gb, p + dx, q)], axis=0)
            g = (gather_dz(mm(kb[...], stack), 96) * mask(p, q)).astype(BF)
            gf[p, q] = mm(g, jz).astype(BF)

    grad_plane(0)
    fsum.two()
    grad_plane(1)
    dsum.three()
    fsum.three()
    dsum.four()
    fsum.four()
    dsum.five()
    fsum.five()
    dsum.six()
    for o in range(27):
        dout[o] = packed(dfull, 192, 14 if o < 9 else 0, o if o < 9 else o - 9)
    fsum.six()
    for j in range(9):
        fout[3 * j : 3 * j + 3] = packed(ffull, 288, 0, j).reshape(3, 96, 96)
    for e in (edge_x, edge_b, edge_g, edge_d):
        e.done()


def local(features, occupancy, w_fine, w_down, cotangent):
    mask = occupancy[0].astype(F32)
    masked = (features[0] * mask).astype(BF)
    xm = jnp.transpose(masked, (1, 2, 0, 3))
    cot = cotangent.reshape(384, 128)
    vm = pl.BlockSpec(memory_space=pltpu.VMEM)

    def sums(h):
        return [
            pltpu.VMEM((32 * h, 128), BF), pltpu.VMEM((32 * h, 128), BF), pltpu.VMEM((16 * h, 128), BF),
            pltpu.VMEM((16 * h, 128), BF), pltpu.VMEM((16, h, 128), BF), pltpu.VMEM((8, h, 128), BF),
        ]

    dma = pltpu.SemaphoreType.DMA
    gf, so, dout, fout = pl.pallas_call(
        kernel,
        out_shape=(
            jax.ShapeDtypeStruct((2, 4, 96, 256), BF),
            jax.ShapeDtypeStruct((384, 128), BF),
            jax.ShapeDtypeStruct((27, 192, 96), BF),
            jax.ShapeDtypeStruct((27, 96, 96), BF),
        ),
        in_specs=[vm] * 5,
        out_specs=(vm,) * 4,
        scratch_shapes=[
            pltpu.VMEM((4, 6, 96, 256), BF),
            pltpu.VMEM((4, 6, 96, 256), BF),
            pltpu.VMEM((18 * 96, 256), BF),
            pltpu.VMEM((2, 4, 96, 256), F32),
            pltpu.VMEM((2, 4, 288, 256), F32),
            pltpu.VMEM((288, 1152), BF),
            pltpu.VMEM((288, 864), BF),
            pltpu.VMEM((3, 192, 864), BF),
            pltpu.VMEM((27, 96, 192), BF),
            pltpu.VMEM((288, 2048), BF),
            pltpu.VMEM((192, 256), BF),
            pltpu.VMEM((192, 256), BF),
            pltpu.VMEM((192, 256), BF),
            pltpu.VMEM((192, 256), BF),
            pltpu.VMEM((2, 4, 96, 256), BF),
        ]
        + sums(HD)
        + sums(HF)
        + [dma((8,)), dma((8,)), dma((56,)), dma((56,)), dma((56,)), dma((56,))],
        compiler_params=pltpu.CompilerParams(
            collective_id=0, has_side_effects=True, vmem_limit_bytes=60 * 2**20
        ),
        name="section",
    )(xm, occupancy[0], w_fine, w_down, cot)
    scale = 1.0 / jnp.sqrt(jnp.float32(65536))
    return (
        so.reshape(1, 192, 1, 2, 128),
        jnp.transpose(gf, (2, 0, 1, 3))[None],
        fout.astype(F32) * scale,
        dout.astype(F32) * scale,
    )


def solution(mesh):
    return jax.shard_map(
        local,
        mesh=mesh,
        in_specs=(
            P("rep", None, "slab", None, None),
            P("rep", "slab", None, None),
            P(),
            P(),
            P("rep", None, "slab", None, None),
        ),
        out_specs=(
            P("rep", None, "slab", None, None),
            P("rep", None, "slab", None, None),
            P(),
            P(),
        ),
        check_vma=False,
    )
```

```python
import jax
import jax.numpy as jnp
from jax import lax
from jax.experimental import pallas as pl
from jax.experimental.pallas import tpu as pltpu
from jax.sharding import PartitionSpec as P

BF = jnp.bfloat16
F32 = jnp.float32
NT = (((1,), (1,)), ((), ()))
HD = 128
HF = 64


def mm(a, b):
    return jnp.dot(a, b, preferred_element_type=F32)


def mm_nt(a, b):
    return lax.dot_general(a, b, NT, preferred_element_type=F32)


def lane_ids(shape):
    return lax.broadcasted_iota(jnp.int32, shape, 1)


def from_before(v):
    return jnp.where(lane_ids(v.shape) == 0, 0.0, pltpu.roll(v, 1, 1))


def from_after(v):
    n = v.shape[1]
    return jnp.where(lane_ids(v.shape) == n - 1, 0.0, pltpu.roll(v, n - 1, 1))


def split_z(n):
    r = lax.broadcasted_iota(jnp.int32, (n, n), 0)
    c = lax.broadcasted_iota(jnp.int32, (n, n), 1)
    src = jnp.where(c < n // 2, 2 * c, 2 * c - n + 1)
    return (r == src).astype(F32).astype(BF)


def join_z(n):
    r = lax.broadcasted_iota(jnp.int32, (n, n), 0)
    c = lax.broadcasted_iota(jnp.int32, (n, n), 1)
    src = jnp.where(r < n // 2, 2 * r, 2 * r - n + 1)
    return (c == src).astype(F32).astype(BF)


def gather_dz(acc, c):
    a0, a1, a2 = acc[:c], acc[c : 2 * c], acc[2 * c :]
    even = from_before(a0[:, 128:]) + a1[:, :128] + a2[:, 128:]
    odd = a0[:, :128] + a1[:, 128:] + from_after(a2[:, :128])
    return jnp.concatenate([even, odd], axis=1)


class Place:
    def __init__(self):
        self.slab = lax.axis_index("slab")
        self.rep = lax.axis_index("rep")
        self.core = self.slab % 2
        self.x = (self.slab // 2) % 4
        self.zlo = self.slab // 8
        self.y = self.rep % 4
        self.zhi = self.rep // 4
        self.z = self.zhi * 4 + self.zlo

    def at(self, core, x, y, z):
        return {"slab": (z % 4) * 8 + x * 2 + core, "rep": (z // 4) * 4 + y}

    def partner(self):
        return self.at(1 - self.core, self.x, self.y, self.z)

    def plane(self, k, sign=1):
        x = (self.x + sign * (k // 4) + 4) % 4
        y = (self.y + sign * (k % 4) + 4) % 4
        return x, y

    def plane_dev(self, k):
        x, y = self.plane(k)
        return self.at(self.core, x, y, self.z)

    def z_dev(self, k):
        return self.at(self.core, self.x, self.y, (self.z + k) % 8)


def remote(src, dst, ssem, rsem, dev):
    return pltpu.make_async_remote_copy(
        src_ref=src, dst_ref=dst, send_sem=ssem, recv_sem=rsem, device_id=dev,
        device_id_type=pl.DeviceIdType.MESH,
    )


class Sum:
    def __init__(self, at, h, cut_z, part, out, cbuf, acc, r1, s2, r2, zb, zr, sems):
        self.at, self.h, self.cut_z = at, h, cut_z
        self.part, self.out, self.cbuf, self.acc = part, out, cbuf, acc
        self.r1, self.s2, self.r2, self.zb, self.zr = r1, s2, r2, zb, zr
        self.ss, self.rr = sems
        self.sent = []
        self.base = at.core * (16 * h)
        self.pos = (at.x, at.y)

    def rows(self, start, n):
        return pl.ds(pl.multiple_of(start, 8), n)

    def copy(self, src, dst, dev):
        i = len(self.sent)
        c = remote(src, dst, self.ss.at[i], self.rr.at[i], dev)
        c.start()
        self.sent.append(c)
        return c

    def along(self, axis, d):
        at = self.at
        x, y = ((at.x + d) % 4, at.y) if axis == 0 else (at.x, (at.y + d) % 4)
        return at.at(at.core, x, y, at.z)

    def one(self):
        src = self.part.at[self.rows((1 - self.at.core) * (16 * self.h), 16 * self.h)]
        self.c1 = self.copy(src, self.cbuf, self.at.partner())

    def two(self):
        self.c1.wait_recv()
        h = self.h
        self.c2 = [[], []]
        for d in (2, 1, 3, 0):
            for axis in range(2):
                start = 8 * h * axis + ((self.pos[axis] + d) % 4) * (2 * h)
                rows = self.rows(start, 2 * h)
                both = self.part[self.rows(self.base + start, 2 * h), :].astype(F32) + self.cbuf[rows, :].astype(F32)
                self.acc[rows, :] = both.astype(BF)
                if d:
                    self.c2[axis].append(self.copy(self.acc.at[rows], self.r1.at[axis, d], self.along(axis, d)))

    def three(self):
        h = self.h
        self.c3 = [[], []]
        for axis in range(2):
            for c in self.c2[axis]:
                c.wait_recv()
            total = self.acc[self.rows(8 * h * axis + self.pos[axis] * (2 * h), 2 * h), :].astype(F32)
            for d in range(1, 4):
                total = total + self.r1[axis, d].astype(F32)
            self.s2[axis] = total.astype(BF)
            for d in (2, 1, 3):
                rows = self.rows(((self.pos[1 - axis] + d) % 4) * (h // 2), h // 2)
                self.c3[axis].append(
                    self.copy(self.s2.at[axis, rows], self.r2.at[axis, d], self.along(1 - axis, d))
                )

    def four(self):
        h, at = self.h, self.at
        for axis in range(2):
            for c in self.c3[axis]:
                c.wait_recv()
            total = self.s2[axis, self.rows(self.pos[1 - axis] * (h // 2), h // 2), :].astype(F32)
            for d in range(1, 4):
                total = total + self.r2[axis, d].astype(F32)
            if self.cut_z:
                self.zr[0, h // 2 * axis : h // 2 * axis + h // 2, :] = total.astype(BF)
            else:
                self.zb[at.z, h // 2 * axis : h // 2 * axis + h // 2, :] = total.astype(BF)
        self.c4 = []
        for k in (4, 3, 5, 2, 6, 1, 7):
            if self.cut_z:
                rows = self.rows(((at.z + k) % 8) * (h // 8), h // 8)
                self.c4.append(self.copy(self.zr.at[0, rows], self.zr.at[k, pl.ds(0, h // 8)], at.z_dev(k)))
            else:
                self.c4.append(self.copy(self.zb.at[at.z], self.zb.at[at.z], at.z_dev(k)))

    def five(self):
        h, at = self.h, self.at
        for c in self.c4:
            c.wait_recv()
        mine = self.rows(at.z * (h // 8), h // 8)
        total = self.zr[0, mine, :].astype(F32)
        for k in range(1, 8):
            total = total + self.zr[k, : h // 8, :].astype(F32)
        self.zb[0, mine, :] = total.astype(BF)
        self.c4 = [
            self.copy(self.zb.at[0, mine], self.zb.at[0, mine], at.z_dev(k)) for k in (4, 3, 5, 2, 6, 1, 7)
        ]

    def block(self, axis, pos):
        return self.rows(self.base + 8 * self.h * axis + pos * (2 * self.h), 2 * self.h)

    def six(self):
        h = self.h
        for c in self.c4:
            c.wait_recv()
        total = self.zb[0].astype(F32)
        if not self.cut_z:
            for k in range(1, 8):
                total = total + self.zb[k].astype(F32)
        self.c6 = [[], []]
        for axis in range(2):
            start = self.base + 8 * h * axis + (self.pos[axis] * 4 + self.pos[1 - axis]) * (h // 2)
            rows = self.rows(start, h // 2)
            self.out[rows, :] = total[h // 2 * axis : h // 2 * axis + h // 2].astype(BF)
            for d in (2, 1, 3):
                self.c6[axis].append(self.copy(self.out.at[rows], self.out.at[rows], self.along(1 - axis, d)))

    def seven(self):
        self.c7, self.c8 = [[], []], []
        for axis in range(2):
            for c in self.c6[axis]:
                c.wait_recv()
            ref = self.out.at[self.block(axis, self.pos[axis])]
            for d in (2, 1, 3):
                self.c7[axis].append((d, self.copy(ref, ref, self.along(axis, d))))
            self.c8.append(self.copy(ref, ref, self.at.partner()))

    def eight(self):
        for i in (1, 2, 0):
            for axis in range(2):
                d, c = self.c7[axis][i]
                c.wait_recv()
                ref = self.out.at[self.block(axis, (self.pos[axis] - d + 4) % 4)]
                self.c8.append(self.copy(ref, ref, self.at.partner()))

    def nine(self):
        for c in self.c8:
            c.wait_recv()
        for c in self.sent:
            c.wait_send()


def packed(ref, rows, tile, slot):
    tile, off = tile + 96 * slot // 128, 96 * slot % 128
    a = ref[rows * tile : rows * tile + rows, :]
    if off == 0:
        return a[:, :96]
    if off == 32:
        return a[:, 32:]
    b = ref[rows * (tile + 1) : rows * (tile + 1) + rows, :]
    return jnp.concatenate([a[:, off:], b[:, : off - 32]], axis=1)


def put_tiles(ref, rows, tile, v):
    extra = -v.shape[1] % 128
    if extra:
        v = jnp.concatenate([v, jnp.zeros((rows, extra), v.dtype)], axis=1)
    for i in range(v.shape[1] // 128):
        ref[rows * (tile + i) : rows * (tile + i) + rows, :] = v[:, 128 * i : 128 * i + 128].astype(BF)


def kernel(
    xf, occ_far, wf_far, wd_far, cot_far,
    gf, so, dout, fout,
    xb, gb, hs, ds, part, kf, kb, kd, kt, gs, gp, gn, bp, bn, raw, rocc, occ, cot, wf, wd, near,
    dpart, dfull, dcb, dacc, dr1, ds2, dr2, dzb, dzr, fpart, ffull, fcb, facc, fr1, fs2, fr2, fzb, fzr,
    hs_s, hs_r, dsem_s, dsem_r, fsem_s, fsem_r,
):
    at = Place()
    first, last = at.slab == 0, at.slab == 31
    left = {"slab": jnp.maximum(at.slab - 1, 0), "rep": at.rep}
    right = {"slab": jnp.minimum(at.slab + 1, 31), "rep": at.rep}
    barrier = pltpu.get_barrier_semaphore()

    def greet(dev):
        pl.semaphore_signal(barrier, 1, device_id=dev, device_id_type=pl.DeviceIdType.MESH)

    @pl.when(jnp.logical_not(first))
    def _():
        greet(left)

    @pl.when(jnp.logical_not(last))
    def _():
        greet(right)

    for k in range(1, 16):
        greet(at.plane_dev(k))
    for k in range(1, 8):
        greet(at.z_dev(k))

    class Edge:
        def __init__(self, i, to_left=None, to_right=None):
            self.l = self.r = None
            if to_left is not None:
                self.l = remote(*to_left, hs_s.at[i], hs_r.at[i], left)
                self.lz = to_left[1]
            if to_right is not None:
                self.r = remote(*to_right, hs_s.at[i + 1], hs_r.at[i + 1], right)
                self.rz = to_right[1]

        def start(self):
            if self.l is not None:
                pl.when(jnp.logical_not(first))(self.l.start)
            if self.r is not None:
                pl.when(jnp.logical_not(last))(self.r.start)

        def from_right(self):
            pl.when(jnp.logical_not(last))(self.l.wait_recv)

            @pl.when(last)
            def _():
                self.lz[...] = jnp.zeros(self.lz.shape, self.lz.dtype)

        def from_left(self):
            pl.when(jnp.logical_not(first))(self.r.wait_recv)

            @pl.when(first)
            def _():
                self.rz[...] = jnp.zeros(self.rz.shape, self.rz.dtype)

        def done(self):
            if self.l is not None:
                pl.when(jnp.logical_not(first))(self.l.wait_send)
            if self.r is not None:
                pl.when(jnp.logical_not(last))(self.r.wait_send)

    inner = (pl.ds(1, 4), slice(None))
    edge_x = Edge(0, (xf.at[0], raw.at[1]), (xf.at[1], raw.at[0]))
    edge_o = Edge(8, (occ_far.at[0], rocc.at[1]), (occ_far.at[1], rocc.at[0]))
    edge_b = Edge(2, to_right=(bp, bn))
    edge_g = Edge(4, to_left=(gp, gn))
    edge_d = Edge(6, (gb.at[(1,) + inner], gb.at[(3,) + inner]), (gb.at[(2,) + inner], gb.at[(0,) + inner]))

    pl.semaphore_wait(barrier, 22 + jnp.where(first, 0, 1) + jnp.where(last, 0, 1))
    edge_o.start()
    edge_x.start()
    pairs = ((occ_far, occ), (wf_far, wf), (wd_far, wd), (cot_far, cot))
    load_o, load_f, load_d, load_c = [
        pltpu.make_async_copy(a, b, near.at[i]) for i, (a, b) in enumerate(pairs)
    ]
    for c in (load_o, load_f, load_d, load_c):
        c.start()

    pz = split_z(256)
    load_o.wait()
    masks = [mm(occ[p].astype(F32).astype(BF), pz) for p in range(2)]
    mask = lambda p, q: masks[p][q : q + 1]
    for p in range(2):
        for q in range(4):
            xb[1 + p, 1 + q] = (mm(xf[p, q], pz) * mask(p, q)).astype(BF)
    for b in (xb, gb):
        for p in range(4):
            b[p, 0] = jnp.zeros((96, 256), BF)
            b[p, 5] = jnp.zeros((96, 256), BF)
    load_f.wait()
    for dx in range(3):
        for dy in range(3):
            base = 384 * dx + 96 * dy
            kf[:, base : base + 96] = wf[9 * dx + 3 * dy : 9 * dx + 3 * dy + 3].reshape(288, 96)
        kf[:, 384 * dx + 288 : 384 * dx + 384] = jnp.zeros((288, 96), BF)

    gap = jnp.zeros((96, 256), BF)

    def rows_of(b, p, q):
        return [b[p, q + dy] for dy in range(3)]

    for p in range(2):
        for q in range(4):
            stack = jnp.concatenate(rows_of(xb, 1, q) + [gap] + rows_of(xb, 2, q), axis=0)
            base = 384 * (1 - p)
            part[p, q] = mm(kf[:, base : base + 672], stack)

    eye = (lax.broadcasted_iota(jnp.int32, (96, 96), 0) == lax.broadcasted_iota(jnp.int32, (96, 96), 1))
    eye = eye.astype(F32).astype(BF)

    def stack_kd(dx):
        for o in range(9 * dx, 9 * dx + 9):
            kd[dx, :, 96 * (o % 9) : 96 * (o % 9) + 96] = wd[o]

    def stack_kt(dx):
        for o in range(9 * dx, 9 * dx + 9):
            kt[o] = mm_nt(eye, wd[o]).astype(BF)

    load_d.wait()
    stack_kd(0)
    stack_kd(1)
    stack_kd(2)

    def finish(p):
        m = mm(rocc[p].astype(F32).astype(BF), pz)
        for q in range(4):
            xb[3 * p, 1 + q] = (mm(raw[p, q], pz) * m[q : q + 1]).astype(BF)
        for q in range(4):
            base = 768 * p
            halo = mm(kf[:, base : base + 288], jnp.concatenate(rows_of(xb, 3 * p, q), axis=0))
            pre = gather_dz(part[p, q] + halo, 96)
            sig = jax.nn.sigmoid(pre)
            h = (pre * sig * mask(p, q)).astype(BF).astype(F32)
            ds[p, q] = mask(p, q) * (sig * (1.0 + pre * (1.0 - sig)))
            even, odd = h[:, :128].astype(BF), h[:, 128:].astype(BF)
            before = from_before(h[:, 128:]).astype(BF)
            for dy in range(3):
                if (q + 1 - dy) % 2 == 0 and 0 <= (q + 1 - dy) // 2 < 2:
                    j = (q + 1 - dy) // 2
                    lanes = slice(128 * j, 128 * j + 128)
                    for dz, v in enumerate((before, even, odd)):
                        row = 96 * (9 * p + 3 * dy + dz)
                        hs[row : row + 96, lanes] = v

    hs_zero = jnp.zeros((288, 128), BF)
    for p in range(2):
        hs[864 * p : 864 * p + 288, :128] = hs_zero
    edge_o.from_right()
    edge_x.from_right()
    finish(1)
    bp[...] = mm(kd[0], hs[864:1728, :]).astype(BF)
    edge_b.start()
    edge_o.from_left()
    edge_x.from_left()
    finish(0)
    down = mm(kd[1], hs[:864, :]) + mm(kd[2], hs[864:1728, :])
    order = join_z(384)
    load_c.wait()
    cots = mm(order, cot[...])
    cots = jnp.concatenate([cots[:192], cots[192:]], axis=1)
    coarse = []
    for j in range(2):
        m = [mask(p, 2 * j + q) for p in range(2) for q in range(2)]
        m = jnp.maximum(jnp.maximum(m[0], m[1]), jnp.maximum(m[2], m[3]))
        coarse.append(jnp.maximum(m[:, :128], m[:, 128:]))
    cm = jnp.concatenate(coarse, axis=1)
    stack_kt(1)
    edge_b.from_left()
    down = down + bn[...].astype(F32)
    sig = jax.nn.sigmoid(down)
    gp[...] = (cots * cm * (sig * (1.0 + down * (1.0 - sig)))).astype(BF)
    edge_g.start()
    stack_kt(2)
    stack_kt(0)
    out = (down * sig * cm).astype(BF)
    out = jnp.concatenate([out[:, :128], out[:, 128:]], axis=0)
    so[...] = mm(split_z(384), out).astype(BF)

    dsum = Sum(at, HD, True, dpart, dfull, dcb, dacc, dr1, ds2, dr2, dzb, dzr, (dsem_s, dsem_r))
    fsum = Sum(at, HF, False, fpart, ffull, fcb, facc, fr1, fs2, fr2, fzb, fzr, (fsem_s, fsem_r))
    for n in range(0, 1728, 768):
        put_tiles(dpart, 192, n // 128, mm_nt(gp[...], hs[n : min(n + 768, 1728), :]))
    dpart[21 * 192 :, :] = jnp.zeros((32 * HD - 21 * 192, 128), BF)

    def back(dx, g):
        r = mm(kt[9 * dx : 9 * dx + 9].reshape(864, 192), g[...])
        out = []
        for q, terms in enumerate((((0, 1),), ((0, 2), (1, 0)), ((1, 1),), ((1, 2),))):
            even, odd = 0.0, 0.0
            for j, dy in terms:
                lanes = slice(128 * j, 128 * j + 128)
                r0, r1, r2 = [r[96 * (3 * dy + dz) : 96 * (3 * dy + dz) + 96, lanes] for dz in range(3)]
                even = even + r1
                odd = odd + r2 + from_after(r0)
            out.append(jnp.concatenate([even, odd], axis=1))
        return out

    for q, v in enumerate(back(1, gp)):
        gb[1, 1 + q] = (v * ds[0, q]).astype(BF)
    own = back(2, gp)
    edge_g.from_right()
    for n in range(0, 864, 768):
        put_tiles(dpart, 192, 14 + n // 128, mm_nt(gn[...], hs[864 + n : 864 + min(n + 768, 864), :]))
    dsum.one()
    nxt = back(0, gn)
    for q in range(4):
        gb[2, 1 + q] = ((own[q] + nxt[q]) * ds[1, q]).astype(BF)
    edge_d.start()

    for p in range(2):
        for q in range(4):
            g = gb[1 + p, 1 + q].astype(F32)
            ge, go = g[:, :128], g[:, 128:]
            base = 256 * (4 * p + q)
            gs[0:96, base : base + 128] = go.astype(BF)
            gs[0:96, base + 128 : base + 256] = from_after(ge).astype(BF)
            gs[96:192, base : base + 256] = g.astype(BF)
            gs[192:288, base : base + 128] = from_before(go).astype(BF)
            gs[192:288, base + 128 : base + 256] = ge.astype(BF)
    for j0 in range(0, 9, 4):
        if j0 == 4:
            dsum.two()
        rhs = jnp.concatenate(
            [
                jnp.concatenate([xb[p + j // 3, q + j % 3] for p in range(2) for q in range(4)], axis=1)
                for j in range(j0, min(j0 + 4, 9))
            ],
            axis=0,
        )
        put_tiles(fpart, 288, 3 * (j0 // 4), mm_nt(gs[...], rhs))
    fpart[7 * 288 :, :] = jnp.zeros((32 * HF - 7 * 288, 128), BF)
    fsum.one()
    for o in range(27):
        kb[96 * (o % 3) : 96 * (o % 3) + 96, 96 * (o // 3) : 96 * (o // 3) + 96] = mm_nt(eye, wf[26 - o]).astype(BF)
    fsum.two()
    dsum.three()
    edge_d.from_right()
    edge_d.from_left()

    jz = join_z(256)

    def grad_plane(p):
        for q in range(4):
            stack = jnp.concatenate([r for dx in range(3) for r in rows_of(gb, p + dx, q)], axis=0)
            g = (gather_dz(mm(kb[...], stack), 96) * mask(p, q)).astype(BF)
            gf[p, q] = mm(g, jz).astype(BF)

    grad_plane(0)
    grad_plane(1)
    dsum.four()
    fsum.three()
    fsum.four()
    dsum.five()
    dsum.six()
    fsum.six()
    dsum.seven()
    fsum.seven()
    dsum.eight()
    fsum.eight()
    dsum.nine()
    for o in range(27):
        dout[o] = packed(dfull, 192, 14 if o < 9 else 0, o if o < 9 else o - 9)
    fsum.nine()
    for j in range(9):
        fout[3 * j : 3 * j + 3] = packed(ffull, 288, 0, j).reshape(3, 96, 96)
    for e in (edge_x, edge_o, edge_b, edge_g, edge_d):
        e.done()


def in_hbm(v):
    return pltpu.with_memory_space_constraint(v, pltpu.HBM)


def local(features, occupancy, w_fine, w_down, cotangent):
    xf = jnp.transpose(features[0], (1, 2, 0, 3))
    cot = cotangent.reshape(384, 128)
    vm = pl.BlockSpec(memory_space=pltpu.VMEM)
    far = pl.BlockSpec(memory_space=pltpu.HBM)

    def sums(h):
        return [
            pltpu.VMEM((32 * h, 128), BF), pltpu.VMEM((32 * h, 128), BF), pltpu.VMEM((16 * h, 128), BF),
            pltpu.VMEM((16 * h, 128), BF), pltpu.VMEM((2, 4, 2 * h, 128), BF), pltpu.VMEM((2, 2 * h, 128), BF),
            pltpu.VMEM((2, 4, h // 2, 128), BF), pltpu.VMEM((8, h, 128), BF), pltpu.VMEM((8, h, 128), BF),
        ]

    dma = pltpu.SemaphoreType.DMA
    gf, so, dout, fout = pl.pallas_call(
        kernel,
        out_shape=(
            jax.ShapeDtypeStruct((2, 4, 96, 256), BF),
            jax.ShapeDtypeStruct((384, 128), BF),
            jax.ShapeDtypeStruct((27, 192, 96), BF),
            jax.ShapeDtypeStruct((27, 96, 96), BF),
        ),
        in_specs=[vm, far, far, far, far],
        out_specs=(vm,) * 4,
        scratch_shapes=[
            pltpu.VMEM((4, 6, 96, 256), BF),
            pltpu.VMEM((4, 6, 96, 256), BF),
            pltpu.VMEM((18 * 96, 256), BF),
            pltpu.VMEM((2, 4, 96, 256), F32),
            pltpu.VMEM((2, 4, 288, 256), F32),
            pltpu.VMEM((288, 1152), BF),
            pltpu.VMEM((288, 864), BF),
            pltpu.VMEM((3, 192, 864), BF),
            pltpu.VMEM((27, 96, 192), BF),
            pltpu.VMEM((288, 2048), BF),
            pltpu.VMEM((192, 256), BF),
            pltpu.VMEM((192, 256), BF),
            pltpu.VMEM((192, 256), BF),
            pltpu.VMEM((192, 256), BF),
            pltpu.VMEM((2, 4, 96, 256), BF),
            pltpu.VMEM((2, 4, 256), jnp.int32),
            pltpu.VMEM((2, 4, 256), jnp.int32),
            pltpu.VMEM((384, 128), BF),
            pltpu.VMEM((27, 96, 96), BF),
            pltpu.VMEM((27, 192, 96), BF),
            dma((4,)),
        ]
        + sums(HD)
        + sums(HF)
        + [dma((10,)), dma((10,)), dma((56,)), dma((56,)), dma((56,)), dma((56,))],
        compiler_params=pltpu.CompilerParams(
            collective_id=0, has_side_effects=True, vmem_limit_bytes=32 * 2**20
        ),
        name="section",
    )(xf, in_hbm(occupancy[0]), in_hbm(w_fine), in_hbm(w_down), in_hbm(cot))
    scale = 1.0 / jnp.sqrt(jnp.float32(65536))
    return (
        so.reshape(1, 192, 1, 2, 128),
        jnp.transpose(gf, (2, 0, 1, 3))[None],
        fout.astype(F32) * scale,
        dout.astype(F32) * scale,
    )


def solution(mesh):
    return jax.shard_map(
        local,
        mesh=mesh,
        in_specs=(
            P("rep", None, "slab", None, None),
            P("rep", "slab", None, None),
            P(),
            P(),
            P("rep", None, "slab", None, None),
        ),
        out_specs=(
            P("rep", None, "slab", None, None),
            P("rep", None, "slab", None, None),
            P(),
            P(),
        ),
        check_vma=False,
    )
```
